256 devices in a mesh: grp: 32 (over x_hi, z, core), rep: 8 (over x_lo, y).
Axes of the slice: x: 4 (x_hi: 2, x_lo: 2; x = x_hi * 2 + x_lo), y: 4, z: 8, core: 2. Of those that a mesh axis runs over, the one named last changes fastest.
Arguments:
- features: bfloat16 [24576, 512], P(('grp', 'rep')), may hold values from -6 to 6
- tile_values: bfloat16 [768, 32, 2, 128, 128], P(('grp', 'rep')), may hold values from 0.019897461 to 1
- tile_columns: int32 [768, 32, 2], P(('grp', 'rep')), may hold values from 0 to 5, as said below
- tile_counts: int32 [768, 32], P(('grp', 'rep')), may hold values from 0 to 2
- state_ids: int32 [98304], P(('grp', 'rep')), may hold values from 0 to 24575
- self_weight: bfloat16 [512, 512], replicated, may hold values from -0.25 to 0.25
- neighbour_weight: bfloat16 [512, 512], replicated, may hold values from -0.25 to 0.25
- bias_vector: float32 [512], replicated, may hold values from -3 to 3
Outputs:
- embedded: bfloat16 [98304, 512], P(('grp', 'rep'))
The draws below stay inside these ranges and needn't reach their ends.
Inputs may be any that keep to these rules, and one draw needn't show every extreme that they name: `tile_columns`: for each row block and group the first tile_counts entries name distinct column blocks of that group; entries beyond the count are padding and are ignored.
All inputs are finite; a program needn't handle non-finite values.
Results may differ from the reference program's by a relative error of at most 0.0033.
Values may be sent and summed in bfloat16 or wider, within the bound.
A program may use at most 192 MiB of HBM per device.

```python
import math
import jax
import jax.numpy as jnp
from jax import lax

F = 512
TILE = 128
SLOTS = 2
PANEL = 768
GROUPS = 32
NODES = 24576
ROWS = 98304
BLOCKS = 768
COLUMN_BLOCKS = 192


def draw_tile_columns(key, part):
    pair_keys = jax.random.split(key, BLOCKS * GROUPS)

    def one_pair(pair_key):
        return jax.random.permutation(pair_key, PANEL // TILE)[:SLOTS]
    return jax.vmap(one_pair)(pair_keys).reshape(BLOCKS, GROUPS, SLOTS).astype(jnp.int32)


def draw_tile_counts(key, part):
    first_key, second_key, third_key = jax.random.split(key, 3)
    loose = jax.random.randint(first_key, (BLOCKS, GROUPS), 0, SLOTS + 1)
    heavy = jax.random.randint(second_key, (BLOCKS, 1), 0, 4) == 0
    counts_all = jnp.where(heavy, SLOTS, loose)
    chosen = jax.random.randint(third_key, (), 0, BLOCKS)
    counts_all = counts_all.at[chosen].set(SLOTS)
    return counts_all.astype(jnp.int32)


def plant(entries, key, least, largest):
    spot = [jax.random.randint(jax.random.fold_in(key, axis), (), 0, length) for axis, length in enumerate(entries.shape)]
    main_axis = entries.shape.index(max(entries.shape))
    beside = spot[:main_axis] + [(spot[main_axis] + 1) % entries.shape[main_axis]] + spot[main_axis + 1:]
    return entries.at[tuple(spot)].set(least).at[tuple(beside)].set(largest)


def level_of(rng, dims, shards, low, high):
    loudness = 1.0
    for position, blocks in shards:
        draws = jax.random.uniform(jax.random.fold_in(jax.random.fold_in(rng, 6), position), (blocks,), jnp.float32, low / len(shards), high / len(shards))
        loudness = loudness * jnp.repeat(jnp.exp(draws), dims[position] // blocks).reshape((-1,) + (1,) * (len(dims) - 1 - position))
    return loudness


def bell_draw(rng, shape, scale, most, cuts=(), kind=jnp.bfloat16):
    values = scale * jax.random.normal(rng, shape, jnp.float32)
    if cuts:
        values = values * level_of(rng, shape, cuts, -0.22, 0.18)
    return jnp.clip(values, -most, most).astype(kind)


def setup_inputs(seed: int = 0) -> dict:
    streams_of = jax.random.split(jax.random.key(seed), 9)
    features = bell_draw(streams_of[0], (NODES, F), 1.0, 6.0, ((0, 256),))
    tile_values = jnp.clip(jnp.exp(math.log(1.0) - 3.9171631 * jax.random.uniform(streams_of[1], (BLOCKS, GROUPS, SLOTS, TILE, TILE), jnp.float32) ** level_of(streams_of[1], (BLOCKS, GROUPS, SLOTS, TILE, TILE), ((0, 256),), -0.2, 0.2)), 0.019897461, 1.0).astype(jnp.bfloat16)
    tile_columns = draw_tile_columns(jax.random.fold_in(streams_of[8], 71), 0)
    tile_counts = draw_tile_counts(jax.random.fold_in(streams_of[8], 71), 0)
    state_ids = plant(jax.random.randint(streams_of[4], (ROWS,), 0, NODES), jax.random.fold_in(streams_of[4], 1), 0, NODES - 1).astype(jnp.int32)
    self_weight = bell_draw(streams_of[5], (F, F), F ** -0.5, 0.25)
    neighbour_weight = bell_draw(streams_of[6], (F, F), F ** -0.5, 0.25)
    bias_vector = bell_draw(streams_of[7], (F,), 0.5, 3.0, (), jnp.float32)
    return {"features": features, "tile_values": tile_values, "tile_columns": tile_columns, "tile_counts": tile_counts, "state_ids": state_ids, "self_weight": self_weight, "neighbour_weight": neighbour_weight, "bias_vector": bias_vector}


def reference(features, tile_values, tile_columns, tile_counts, state_ids, self_weight, neighbour_weight, bias_vector):
    column_blocks = features.reshape(COLUMN_BLOCKS, TILE, F)
    positions = jnp.arange(SLOTS, dtype=jnp.int32)
    group_first = jnp.arange(GROUPS, dtype=jnp.int32) * (PANEL // TILE)

    def one_block(packed):
        values, columns, counts = packed
        usable = positions[None, :] < counts[:, None]
        global_blocks = (group_first[:, None] + columns.astype(jnp.int32)).reshape(GROUPS * SLOTS)
        picked = jnp.take(column_blocks, global_blocks, axis=0).astype(jnp.float32)
        picked = picked.reshape(GROUPS, SLOTS, TILE, F)
        masked = jnp.where(usable[:, :, None, None], values.astype(jnp.float32), jnp.float32(0.0))
        summed = jnp.einsum('gsij,gsjf->if', masked, picked)
        degree = 1.0 + lax.optimization_barrier(jnp.sum(masked, axis=(0, 1, 3)))
        return (summed / jnp.sqrt(degree)[:, None]).astype(jnp.bfloat16)
    neighbour = lax.map(one_block, (tile_values, tile_columns, tile_counts)).reshape(ROWS, F)
    own_rows = jnp.take(features, state_ids.astype(jnp.int32), axis=0)
    activation = jnp.dot(own_rows, self_weight, preferred_element_type=jnp.float32)
    activation = activation + jnp.dot(neighbour, neighbour_weight, preferred_element_type=jnp.float32)
    activation = activation + bias_vector[None, :]
    return jnp.maximum(activation, 0.0).astype(jnp.bfloat16)
```

```python
import jax
import jax.numpy as jnp
from jax import lax
from jax.sharding import PartitionSpec as P


def on_device(
    features,
    tile_values,
    tile_columns,
    tile_counts,
    state_ids,
    self_weight,
    neighbour_weight,
    bias_vector,
):
    panels = lax.all_gather(features, "rep", axis=0, tiled=True)
    everything = lax.all_gather(panels, "grp", axis=0, tiled=True)
    row_blocks, group_count, slot_count, tile_size, _ = tile_values.shape
    panel_rows = panels.shape[0]
    panel_blocks = panel_rows // tile_size
    local_rows = row_blocks * tile_size
    total_rows = everything.shape[0]

    positions = lax.broadcasted_iota(jnp.int32, (row_blocks, group_count, slot_count), 2)
    usable = positions < tile_counts[:, :, None]
    row_sums = jnp.sum(tile_values, axis=4, dtype=jnp.float32)
    degree = 1.0 + jnp.sum(
        jnp.where(usable[:, :, :, None], row_sums, jnp.float32(0.0)), axis=(1, 2)
    ).reshape(local_rows)

    block_iota = lax.broadcasted_iota(jnp.int32, (1, 1, 1, panel_blocks), 3)
    hits = (tile_columns[:, :, :, None] == block_iota) & usable[:, :, :, None]
    by_row = jnp.transpose(tile_values, (0, 3, 1, 2, 4))
    dense = jnp.zeros((row_blocks, tile_size, group_count, panel_blocks, tile_size), jnp.bfloat16)
    for slot in range(slot_count):
        dense = jnp.where(
            hits[:, None, :, slot, :, None], by_row[:, :, :, slot, None, :], dense
        )
    dense = dense.reshape(local_rows, total_rows)

    totals = jnp.dot(dense, everything, preferred_element_type=jnp.float32)
    own_rows = jnp.take(everything, state_ids, axis=0)
    neighbour = (totals / jnp.sqrt(degree)[:, None]).astype(jnp.bfloat16)
    activation = jnp.dot(own_rows, self_weight, preferred_element_type=jnp.float32)
    activation = activation + jnp.dot(
        neighbour, neighbour_weight, preferred_element_type=jnp.float32
    )
    activation = activation + bias_vector[None, :]
    return jnp.maximum(activation, 0.0).astype(jnp.bfloat16)


def solution(mesh):
    placed = (
        P(("grp", "rep"), None),
        P(("grp", "rep"), None, None, None, None),
        P(("grp", "rep"), None, None),
        P(("grp", "rep"), None),
        P(("grp", "rep")),
        P(),
        P(),
        P(),
    )
    return jax.shard_map(
        on_device, mesh=mesh, in_specs=placed, out_specs=P(("grp", "rep"), None), check_vma=False
    )
```

```python
import functools

import jax
import jax.numpy as jnp
from jax import lax
from jax.experimental import pallas as pl
from jax.experimental.pallas import tpu as pltpu
from jax.sharding import PartitionSpec as P


def rep_gather_kernel(count, x_ref, o_ref, send_sem, recv_sem):
    me = lax.axis_index("rep")
    team = lax.axis_index("grp")
    rows = x_ref.shape[0]
    mesh_id = pl.DeviceIdType.MESH
    barrier = pltpu.get_barrier_semaphore()
    for step in range(1, count):
        peer = lax.rem(me + step, count)
        pl.semaphore_signal(barrier, inc=1, device_id=(team, peer), device_id_type=mesh_id)
    pl.semaphore_wait(barrier, count - 1)
    sends = []
    for step in range(1, count):
        peer = lax.rem(me + step, count)
        copy = pltpu.make_async_remote_copy(
            src_ref=x_ref,
            dst_ref=o_ref.at[pl.ds(pl.multiple_of(me * rows, rows), rows)],
            send_sem=send_sem.at[step],
            recv_sem=recv_sem.at[step],
            device_id=(team, peer),
            device_id_type=mesh_id,
        )
        copy.start()
        sends.append(copy)
    o_ref[pl.ds(pl.multiple_of(me * rows, rows), rows), :] = x_ref[...]
    for step in range(1, count):
        source = lax.rem(me + count - step, count)
        arriving = pltpu.make_async_remote_copy(
            src_ref=x_ref,
            dst_ref=o_ref.at[pl.ds(pl.multiple_of(source * rows, rows), rows)],
            send_sem=send_sem.at[step],
            recv_sem=recv_sem.at[step],
            device_id=(team, source),
            device_id_type=mesh_id,
        )
        arriving.wait_recv()
    for copy in sends:
        copy.wait_send()


def rep_gather(x, count):
    rows, width = x.shape
    return pl.pallas_call(
        functools.partial(rep_gather_kernel, count),
        out_shape=jax.ShapeDtypeStruct((rows * count, width), x.dtype),
        in_specs=[pl.BlockSpec(memory_space=pltpu.VMEM)],
        out_specs=pl.BlockSpec(memory_space=pltpu.VMEM),
        scratch_shapes=[
            pltpu.SemaphoreType.DMA((count,)),
            pltpu.SemaphoreType.DMA((count,)),
        ],
        compiler_params=pltpu.CompilerParams(collective_id=0, has_side_effects=True),
    )(x)


def on_device(
    features,
    tile_values,
    tile_columns,
    tile_counts,
    state_ids,
    self_weight,
    neighbour_weight,
    bias_vector,
):
    panels = rep_gather(features, REP_COUNT[0])
    everything = lax.all_gather(panels, "grp", axis=0, tiled=True)
    row_blocks, group_count, slot_count, tile_size, _ = tile_values.shape
    panel_rows = panels.shape[0]
    panel_blocks = panel_rows // tile_size
    local_rows = row_blocks * tile_size
    total_rows = everything.shape[0]

    positions = lax.broadcasted_iota(jnp.int32, (row_blocks, group_count, slot_count), 2)
    usable = positions < tile_counts[:, :, None]
    row_sums = jnp.sum(tile_values, axis=4, dtype=jnp.float32)
    degree = 1.0 + jnp.sum(
        jnp.where(usable[:, :, :, None], row_sums, jnp.float32(0.0)), axis=(1, 2)
    ).reshape(local_rows)

    block_iota = lax.broadcasted_iota(jnp.int32, (1, 1, 1, panel_blocks), 3)
    hits = (tile_columns[:, :, :, None] == block_iota) & usable[:, :, :, None]
    by_row = jnp.transpose(tile_values, (0, 3, 1, 2, 4))
    dense = jnp.zeros((row_blocks, tile_size, group_count, panel_blocks, tile_size), jnp.bfloat16)
    for slot in range(slot_count):
        dense = jnp.where(
            hits[:, None, :, slot, :, None], by_row[:, :, :, slot, None, :], dense
        )
    dense = dense.reshape(local_rows, total_rows)

    totals = jnp.dot(dense, everything, preferred_element_type=jnp.float32)
    own_rows = jnp.take(everything, state_ids, axis=0)
    neighbour = (totals / jnp.sqrt(degree)[:, None]).astype(jnp.bfloat16)
    activation = jnp.dot(own_rows, self_weight, preferred_element_type=jnp.float32)
    activation = activation + jnp.dot(
        neighbour, neighbour_weight, preferred_element_type=jnp.float32
    )
    activation = activation + bias_vector[None, :]
    return jnp.maximum(activation, 0.0).astype(jnp.bfloat16)


REP_COUNT = [8]


def solution(mesh):
    REP_COUNT[0] = mesh.shape["rep"]
    placed = (
        P(("grp", "rep"), None),
        P(("grp", "rep"), None, None, None, None),
        P(("grp", "rep"), None, None),
        P(("grp", "rep"), None),
        P(("grp", "rep")),
        P(),
        P(),
        P(),
    )
    return jax.shard_map(
        on_device, mesh=mesh, in_specs=placed, out_specs=P(("grp", "rep"), None), check_vma=False
    )
```

```python
import functools

import jax
import jax.numpy as jnp
from jax import lax
from jax.experimental import pallas as pl
from jax.experimental.pallas import tpu as pltpu
from jax.sharding import PartitionSpec as P


def rep_gather_kernel(count, x_ref, o_ref, send_sem, recv_sem):
    me = lax.axis_index("rep")
    team = lax.axis_index("grp")
    rows = x_ref.shape[0]
    mesh_id = pl.DeviceIdType.MESH
    barrier = pltpu.get_barrier_semaphore()
    for step in range(1, count):
        peer = lax.rem(me + step, count)
        pl.semaphore_signal(barrier, inc=1, device_id=(team, peer), device_id_type=mesh_id)
    pl.semaphore_wait(barrier, count - 1)
    sends = []
    for step in range(1, count):
        peer = lax.rem(me + step, count)
        copy = pltpu.make_async_remote_copy(
            src_ref=x_ref,
            dst_ref=o_ref.at[pl.ds(pl.multiple_of(me * rows, rows), rows)],
            send_sem=send_sem.at[step],
            recv_sem=recv_sem.at[step],
            device_id=(team, peer),
            device_id_type=mesh_id,
        )
        copy.start()
        sends.append(copy)
    o_ref[pl.ds(pl.multiple_of(me * rows, rows), rows), :] = x_ref[...]
    for step in range(1, count):
        source = lax.rem(me + count - step, count)
        arriving = pltpu.make_async_remote_copy(
            src_ref=x_ref,
            dst_ref=o_ref.at[pl.ds(pl.multiple_of(source * rows, rows), rows)],
            send_sem=send_sem.at[step],
            recv_sem=recv_sem.at[step],
            device_id=(team, source),
            device_id_type=mesh_id,
        )
        arriving.wait_recv()
    for copy in sends:
        copy.wait_send()


def row_gather_kernel(ids_ref, table_ref, out_ref, sem):
    count = ids_ref.shape[0]
    last = table_ref.shape[0] - 1

    def issue(r, carry):
        row = jnp.minimum(jnp.maximum(ids_ref[r], 0), last)
        start = pl.multiple_of((row // 2) * 2, 2)
        pltpu.make_async_copy(
            table_ref.at[pl.ds(start, 2)], out_ref.at[pl.ds(pl.multiple_of(r * 2, 2), 2)], sem
        ).start()
        return carry

    lax.fori_loop(0, count, issue, 0)
    pltpu.make_async_copy(table_ref.at[pl.ds(0, 2 * count)], out_ref, sem).wait()


def row_gather(table, ids):
    count, width = ids.shape[0], table.shape[1]
    pairs = pl.pallas_call(
        row_gather_kernel,
        out_shape=jax.ShapeDtypeStruct((2 * count, width), table.dtype),
        in_specs=[
            pl.BlockSpec(memory_space=pltpu.SMEM),
            pl.BlockSpec(memory_space=pl.ANY),
        ],
        out_specs=pl.BlockSpec(memory_space=pltpu.VMEM),
        scratch_shapes=[pltpu.SemaphoreType.DMA(())],
    )(ids, table).reshape(count, 2, width)
    odd = (ids % 2 == 1)[:, None]
    return jnp.where(odd, pairs[:, 1, :], pairs[:, 0, :])


def rep_gather(x, count):
    rows, width = x.shape
    return pl.pallas_call(
        functools.partial(rep_gather_kernel, count),
        out_shape=jax.ShapeDtypeStruct((rows * count, width), x.dtype),
        in_specs=[pl.BlockSpec(memory_space=pltpu.VMEM)],
        out_specs=pl.BlockSpec(memory_space=pltpu.VMEM),
        scratch_shapes=[
            pltpu.SemaphoreType.DMA((count,)),
            pltpu.SemaphoreType.DMA((count,)),
        ],
        compiler_params=pltpu.CompilerParams(collective_id=0, has_side_effects=True),
    )(x)


def on_device(
    features,
    tile_values,
    tile_columns,
    tile_counts,
    state_ids,
    self_weight,
    neighbour_weight,
    bias_vector,
):
    panels = rep_gather(features, REP_COUNT[0])
    everything = lax.all_gather(panels, "grp", axis=0, tiled=True)
    row_blocks, group_count, slot_count, tile_size, _ = tile_values.shape
    panel_rows = panels.shape[0]
    panel_blocks = panel_rows // tile_size
    local_rows = row_blocks * tile_size
    total_rows = everything.shape[0]

    positions = lax.broadcasted_iota(jnp.int32, (row_blocks, group_count, slot_count), 2)
    usable = positions < tile_counts[:, :, None]
    row_sums = jnp.sum(tile_values, axis=4, dtype=jnp.float32)
    degree = 1.0 + jnp.sum(
        jnp.where(usable[:, :, :, None], row_sums, jnp.float32(0.0)), axis=(1, 2)
    ).reshape(local_rows)

    block_iota = lax.broadcasted_iota(jnp.int32, (1, 1, 1, panel_blocks), 3)
    hits = (tile_columns[:, :, :, None] == block_iota) & usable[:, :, :, None]
    by_row = jnp.transpose(tile_values, (0, 3, 1, 2, 4))
    dense = jnp.zeros((row_blocks, tile_size, group_count, panel_blocks, tile_size), jnp.bfloat16)
    for slot in range(slot_count):
        dense = jnp.where(
            hits[:, None, :, slot, :, None], by_row[:, :, :, slot, None, :], dense
        )
    dense = dense.reshape(local_rows, total_rows)

    totals = jnp.dot(dense, everything, preferred_element_type=jnp.float32)
    own_rows = row_gather(everything, state_ids)
    neighbour = (totals / jnp.sqrt(degree)[:, None]).astype(jnp.bfloat16)
    activation = jnp.dot(own_rows, self_weight, preferred_element_type=jnp.float32)
    activation = activation + jnp.dot(
        neighbour, neighbour_weight, preferred_element_type=jnp.float32
    )
    activation = activation + bias_vector[None, :]
    return jnp.maximum(activation, 0.0).astype(jnp.bfloat16)


REP_COUNT = [8]


def solution(mesh):
    REP_COUNT[0] = mesh.shape["rep"]
    placed = (
        P(("grp", "rep"), None),
        P(("grp", "rep"), None, None, None, None),
        P(("grp", "rep"), None, None),
        P(("grp", "rep"), None),
        P(("grp", "rep")),
        P(),
        P(),
        P(),
    )
    return jax.shard_map(
        on_device, mesh=mesh, in_specs=placed, out_specs=P(("grp", "rep"), None), check_vma=False
    )
```

```python
import functools

import jax
import jax.numpy as jnp
from jax import lax
from jax.experimental import pallas as pl
from jax.experimental.pallas import tpu as pltpu
from jax.sharding import PartitionSpec as P


def rep_gather_kernel(count, x_ref, o_ref, send_sem, recv_sem):
    me = lax.axis_index("rep")
    team = lax.axis_index("grp")
    rows = x_ref.shape[0]
    mesh_id = pl.DeviceIdType.MESH
    barrier = pltpu.get_barrier_semaphore()
    for step in range(1, count):
        peer = lax.rem(me + step, count)
        pl.semaphore_signal(barrier, inc=1, device_id=(team, peer), device_id_type=mesh_id)
    pl.semaphore_wait(barrier, count - 1)
    sends = []
    for step in range(1, count):
        peer = lax.rem(me + step, count)
        copy = pltpu.make_async_remote_copy(
            src_ref=x_ref,
            dst_ref=o_ref.at[pl.ds(pl.multiple_of(me * rows, rows), rows)],
            send_sem=send_sem.at[step],
            recv_sem=recv_sem.at[step],
            device_id=(team, peer),
            device_id_type=mesh_id,
        )
        copy.start()
        sends.append(copy)
    o_ref[pl.ds(pl.multiple_of(me * rows, rows), rows), :] = x_ref[...]
    for step in range(1, count):
        source = lax.rem(me + count - step, count)
        arriving = pltpu.make_async_remote_copy(
            src_ref=x_ref,
            dst_ref=o_ref.at[pl.ds(pl.multiple_of(source * rows, rows), rows)],
            send_sem=send_sem.at[step],
            recv_sem=recv_sem.at[step],
            device_id=(team, source),
            device_id_type=mesh_id,
        )
        arriving.wait_recv()
    for copy in sends:
        copy.wait_send()


def row_gather_kernel(ids_ref, table_ref, out_ref, sem):
    count = ids_ref.shape[0]
    last = table_ref.shape[0] - 1

    def issue(r, carry):
        row = jnp.minimum(jnp.maximum(ids_ref[r], 0), last)
        start = pl.multiple_of((row // 2) * 2, 2)
        pltpu.make_async_copy(
            table_ref.at[pl.ds(start, 2)], out_ref.at[pl.ds(pl.multiple_of(r * 2, 2), 2)], sem
        ).start()
        return carry

    lax.fori_loop(0, count, issue, 0, unroll=16)
    pltpu.make_async_copy(table_ref.at[pl.ds(0, 2 * count)], out_ref, sem).wait()


def row_gather(table, ids):
    count, width = ids.shape[0], table.shape[1]
    pairs = pl.pallas_call(
        row_gather_kernel,
        out_shape=jax.ShapeDtypeStruct((2 * count, width), table.dtype),
        in_specs=[
            pl.BlockSpec(memory_space=pltpu.SMEM),
            pl.BlockSpec(memory_space=pl.ANY),
        ],
        out_specs=pl.BlockSpec(memory_space=pltpu.VMEM),
        scratch_shapes=[pltpu.SemaphoreType.DMA(())],
    )(ids, table).reshape(count, 2, width)
    odd = (ids % 2 == 1)[:, None]
    return jnp.where(odd, pairs[:, 1, :], pairs[:, 0, :])


def rep_gather(x, count):
    rows, width = x.shape
    return pl.pallas_call(
        functools.partial(rep_gather_kernel, count),
        out_shape=jax.ShapeDtypeStruct((rows * count, width), x.dtype),
        in_specs=[pl.BlockSpec(memory_space=pltpu.VMEM)],
        out_specs=pl.BlockSpec(memory_space=pltpu.VMEM),
        scratch_shapes=[
            pltpu.SemaphoreType.DMA((count,)),
            pltpu.SemaphoreType.DMA((count,)),
        ],
        compiler_params=pltpu.CompilerParams(collective_id=0, has_side_effects=True),
    )(x)


def on_device(
    features,
    tile_values,
    tile_columns,
    tile_counts,
    state_ids,
    self_weight,
    neighbour_weight,
    bias_vector,
):
    panels = rep_gather(features, REP_COUNT[0])
    everything = lax.all_gather(panels, "grp", axis=0, tiled=True)
    row_blocks, group_count, slot_count, tile_size, _ = tile_values.shape
    panel_rows = panels.shape[0]
    panel_blocks = panel_rows // tile_size
    local_rows = row_blocks * tile_size
    total_rows = everything.shape[0]

    positions = lax.broadcasted_iota(jnp.int32, (row_blocks, group_count, slot_count), 2)
    usable = positions < tile_counts[:, :, None]
    row_sums = jnp.sum(tile_values, axis=4, dtype=jnp.float32)
    degree = 1.0 + jnp.sum(
        jnp.where(usable[:, :, :, None], row_sums, jnp.float32(0.0)), axis=(1, 2)
    ).reshape(local_rows)

    block_iota = lax.broadcasted_iota(jnp.int32, (1, 1, 1, panel_blocks), 3)
    hits = (tile_columns[:, :, :, None] == block_iota) & usable[:, :, :, None]
    by_row = jnp.transpose(tile_values, (0, 3, 1, 2, 4))
    dense = jnp.zeros((row_blocks, tile_size, group_count, panel_blocks, tile_size), jnp.bfloat16)
    for slot in range(slot_count):
        dense = jnp.where(
            hits[:, None, :, slot, :, None], by_row[:, :, :, slot, None, :], dense
        )
    dense = dense.reshape(local_rows, total_rows)

    totals = jnp.dot(dense, everything, preferred_element_type=jnp.float32)
    own_rows = row_gather(everything, state_ids)
    neighbour = (totals / jnp.sqrt(degree)[:, None]).astype(jnp.bfloat16)
    activation = jnp.dot(own_rows, self_weight, preferred_element_type=jnp.float32)
    activation = activation + jnp.dot(
        neighbour, neighbour_weight, preferred_element_type=jnp.float32
    )
    activation = activation + bias_vector[None, :]
    return jnp.maximum(activation, 0.0).astype(jnp.bfloat16)


REP_COUNT = [8]


def solution(mesh):
    REP_COUNT[0] = mesh.shape["rep"]
    placed = (
        P(("grp", "rep"), None),
        P(("grp", "rep"), None, None, None, None),
        P(("grp", "rep"), None, None),
        P(("grp", "rep"), None),
        P(("grp", "rep")),
        P(),
        P(),
        P(),
    )
    return jax.shard_map(
        on_device, mesh=mesh, in_specs=placed, out_specs=P(("grp", "rep"), None), check_vma=False
    )
```

```python
import functools

import jax
import jax.numpy as jnp
from jax import lax
from jax.experimental import pallas as pl
from jax.experimental.pallas import tpu as pltpu
from jax.sharding import PartitionSpec as P


def rep_gather_kernel(count, x_ref, o_ref, send_sem, recv_sem):
    me = lax.axis_index("rep")
    team = lax.axis_index("grp")
    rows = x_ref.shape[0]
    mesh_id = pl.DeviceIdType.MESH
    barrier = pltpu.get_barrier_semaphore()
    for step in range(1, count):
        peer = lax.rem(me + step, count)
        pl.semaphore_signal(barrier, inc=1, device_id=(team, peer), device_id_type=mesh_id)
    pl.semaphore_wait(barrier, count - 1)
    sends = []
    for step in range(1, count):
        peer = lax.rem(me + step, count)
        copy = pltpu.make_async_remote_copy(
            src_ref=x_ref,
            dst_ref=o_ref.at[pl.ds(pl.multiple_of(me * rows, rows), rows)],
            send_sem=send_sem.at[step],
            recv_sem=recv_sem.at[step],
            device_id=(team, peer),
            device_id_type=mesh_id,
        )
        copy.start()
        sends.append(copy)
    o_ref[pl.ds(pl.multiple_of(me * rows, rows), rows), :] = x_ref[...]
    for step in range(1, count):
        source = lax.rem(me + count - step, count)
        arriving = pltpu.make_async_remote_copy(
            src_ref=x_ref,
            dst_ref=o_ref.at[pl.ds(pl.multiple_of(source * rows, rows), rows)],
            send_sem=send_sem.at[step],
            recv_sem=recv_sem.at[step],
            device_id=(team, source),
            device_id_type=mesh_id,
        )
        arriving.wait_recv()
    for copy in sends:
        copy.wait_send()


def product_kernel(ids_ref, a_ref, f_ref, table_ref, tot_ref, pairs_ref, sem):
    step = pl.program_id(0)
    count = ids_ref.shape[0]
    last = table_ref.shape[0] - 1

    def issue(r, carry):
        row = jnp.minimum(jnp.maximum(ids_ref[r], 0), last)
        start = pl.multiple_of((row // 2) * 2, 2)
        pltpu.make_async_copy(
            table_ref.at[pl.ds(start, 2)], pairs_ref.at[pl.ds(pl.multiple_of(r * 2, 2), 2)], sem
        ).start()
        return carry

    @pl.when(step == 0)
    def _():
        tot_ref[...] = jnp.zeros_like(tot_ref)
        lax.fori_loop(0, count, issue, 0, unroll=16)

    tot_ref[...] += jnp.dot(a_ref[...], f_ref[...], preferred_element_type=jnp.float32)

    @pl.when(step == pl.num_programs(0) - 1)
    def _():
        pltpu.make_async_copy(table_ref.at[pl.ds(0, 2 * count)], pairs_ref, sem).wait()


def product_and_rows(dense, table, ids, depth=2048):
    rows, inner = dense.shape
    count, width = ids.shape[0], table.shape[1]
    totals, pairs = pl.pallas_call(
        product_kernel,
        out_shape=(
            jax.ShapeDtypeStruct((rows, width), jnp.float32),
            jax.ShapeDtypeStruct((2 * count, width), table.dtype),
        ),
        grid_spec=pltpu.PrefetchScalarGridSpec(
            num_scalar_prefetch=1,
            grid=(inner // depth,),
            in_specs=[
                pl.BlockSpec((rows, depth), lambda k, ids: (0, k)),
                pl.BlockSpec((depth, width), lambda k, ids: (k, 0)),
                pl.BlockSpec(memory_space=pl.ANY),
            ],
            out_specs=[
                pl.BlockSpec((rows, width), lambda k, ids: (0, 0)),
                pl.BlockSpec((2 * count, width), lambda k, ids: (0, 0)),
            ],
            scratch_shapes=[pltpu.SemaphoreType.DMA(())],
        ),
        compiler_params=pltpu.CompilerParams(dimension_semantics=("arbitrary",)),
        cost_estimate=pl.CostEstimate(
            flops=2 * rows * inner * width,
            bytes_accessed=2 * (rows * inner + inner * width),
            transcendentals=0,
        ),
    )(ids, dense, table, table)
    pairs = pairs.reshape(count, 2, width)
    odd = (ids % 2 == 1)[:, None]
    return totals, jnp.where(odd, pairs[:, 1, :], pairs[:, 0, :])


def rep_gather(x, count):
    rows, width = x.shape
    return pl.pallas_call(
        functools.partial(rep_gather_kernel, count),
        out_shape=jax.ShapeDtypeStruct((rows * count, width), x.dtype),
        in_specs=[pl.BlockSpec(memory_space=pltpu.VMEM)],
        out_specs=pl.BlockSpec(memory_space=pltpu.VMEM),
        scratch_shapes=[
            pltpu.SemaphoreType.DMA((count,)),
            pltpu.SemaphoreType.DMA((count,)),
        ],
        compiler_params=pltpu.CompilerParams(collective_id=0, has_side_effects=True),
    )(x)


def on_device(
    features,
    tile_values,
    tile_columns,
    tile_counts,
    state_ids,
    self_weight,
    neighbour_weight,
    bias_vector,
):
    panels = rep_gather(features, REP_COUNT[0])
    everything = lax.all_gather(panels, "grp", axis=0, tiled=True)
    row_blocks, group_count, slot_count, tile_size, _ = tile_values.shape
    panel_rows = panels.shape[0]
    panel_blocks = panel_rows // tile_size
    local_rows = row_blocks * tile_size
    total_rows = everything.shape[0]

    positions = lax.broadcasted_iota(jnp.int32, (row_blocks, group_count, slot_count), 2)
    usable = positions < tile_counts[:, :, None]
    row_sums = jnp.sum(tile_values, axis=4, dtype=jnp.float32)
    degree = 1.0 + jnp.sum(
        jnp.where(usable[:, :, :, None], row_sums, jnp.float32(0.0)), axis=(1, 2)
    ).reshape(local_rows)

    block_iota = lax.broadcasted_iota(jnp.int32, (1, 1, 1, panel_blocks), 3)
    hits = (tile_columns[:, :, :, None] == block_iota) & usable[:, :, :, None]
    by_row = jnp.transpose(tile_values, (0, 3, 1, 2, 4))
    dense = jnp.zeros((row_blocks, tile_size, group_count, panel_blocks, tile_size), jnp.bfloat16)
    for slot in range(slot_count):
        dense = jnp.where(
            hits[:, None, :, slot, :, None], by_row[:, :, :, slot, None, :], dense
        )
    dense = dense.reshape(local_rows, total_rows)

    totals, own_rows = product_and_rows(dense, everything, state_ids)
    neighbour = (totals / jnp.sqrt(degree)[:, None]).astype(jnp.bfloat16)
    activation = jnp.dot(own_rows, self_weight, preferred_element_type=jnp.float32)
    activation = activation + jnp.dot(
        neighbour, neighbour_weight, preferred_element_type=jnp.float32
    )
    activation = activation + bias_vector[None, :]
    return jnp.maximum(activation, 0.0).astype(jnp.bfloat16)


REP_COUNT = [8]


def solution(mesh):
    REP_COUNT[0] = mesh.shape["rep"]
    placed = (
        P(("grp", "rep"), None),
        P(("grp", "rep"), None, None, None, None),
        P(("grp", "rep"), None, None),
        P(("grp", "rep"), None),
        P(("grp", "rep")),
        P(),
        P(),
        P(),
    )
    return jax.shard_map(
        on_device, mesh=mesh, in_specs=placed, out_specs=P(("grp", "rep"), None), check_vma=False
    )
```

```python
import functools

import jax
import jax.numpy as jnp
from jax import lax
from jax.experimental import pallas as pl
from jax.experimental.pallas import tpu as pltpu
from jax.sharding import PartitionSpec as P


def rep_gather_kernel(count, x_ref, o_ref, send_sem, recv_sem):
    me = lax.axis_index("rep")
    team = lax.axis_index("grp")
    rows = x_ref.shape[0]
    mesh_id = pl.DeviceIdType.MESH
    barrier = pltpu.get_barrier_semaphore()
    for step in range(1, count):
        peer = lax.rem(me + step, count)
        pl.semaphore_signal(barrier, inc=1, device_id=(team, peer), device_id_type=mesh_id)
    pl.semaphore_wait(barrier, count - 1)
    sends = []
    for step in range(1, count):
        peer = lax.rem(me + step, count)
        copy = pltpu.make_async_remote_copy(
            src_ref=x_ref,
            dst_ref=o_ref.at[pl.ds(pl.multiple_of(me * rows, rows), rows)],
            send_sem=send_sem.at[step],
            recv_sem=recv_sem.at[step],
            device_id=(team, peer),
            device_id_type=mesh_id,
        )
        copy.start()
        sends.append(copy)
    o_ref[pl.ds(pl.multiple_of(me * rows, rows), rows), :] = x_ref[...]
    for step in range(1, count):
        source = lax.rem(me + count - step, count)
        arriving = pltpu.make_async_remote_copy(
            src_ref=x_ref,
            dst_ref=o_ref.at[pl.ds(pl.multiple_of(source * rows, rows), rows)],
            send_sem=send_sem.at[step],
            recv_sem=recv_sem.at[step],
            device_id=(team, source),
            device_id_type=mesh_id,
        )
        arriving.wait_recv()
    for copy in sends:
        copy.wait_send()


def row_gather_kernel(ids_ref, table_ref, out_ref, sem):
    count = ids_ref.shape[0]
    last = table_ref.shape[0] - 1

    def issue(r, carry):
        row = jnp.minimum(jnp.maximum(ids_ref[r], 0), last)
        start = pl.multiple_of((row // 2) * 2, 2)
        pltpu.make_async_copy(
            table_ref.at[pl.ds(start, 2)], out_ref.at[pl.ds(pl.multiple_of(r * 2, 2), 2)], sem
        ).start()
        return carry

    lax.fori_loop(0, count, issue, 0, unroll=16)
    pltpu.make_async_copy(table_ref.at[pl.ds(0, 2 * count)], out_ref, sem).wait()


def row_gather(table, ids):
    count, width = ids.shape[0], table.shape[1]
    pairs = pl.pallas_call(
        row_gather_kernel,
        out_shape=jax.ShapeDtypeStruct((2 * count, width), table.dtype),
        in_specs=[
            pl.BlockSpec(memory_space=pltpu.SMEM),
            pl.BlockSpec(memory_space=pl.ANY),
        ],
        out_specs=pl.BlockSpec(memory_space=pltpu.VMEM),
        scratch_shapes=[pltpu.SemaphoreType.DMA(())],
    )(ids, table)
    wanted = 2 * lax.broadcasted_iota(jnp.int32, (count, 1), 0) + (ids % 2)[:, None]
    picks = (lax.broadcasted_iota(jnp.int32, (count, 2 * count), 1) == wanted).astype(table.dtype)
    return jnp.dot(picks, pairs, preferred_element_type=jnp.float32).astype(table.dtype)


def rep_gather(x, count):
    rows, width = x.shape
    return pl.pallas_call(
        functools.partial(rep_gather_kernel, count),
        out_shape=jax.ShapeDtypeStruct((rows * count, width), x.dtype),
        in_specs=[pl.BlockSpec(memory_space=pltpu.VMEM)],
        out_specs=pl.BlockSpec(memory_space=pltpu.VMEM),
        scratch_shapes=[
            pltpu.SemaphoreType.DMA((count,)),
            pltpu.SemaphoreType.DMA((count,)),
        ],
        compiler_params=pltpu.CompilerParams(collective_id=0, has_side_effects=True),
    )(x)


def on_device(
    features,
    tile_values,
    tile_columns,
    tile_counts,
    state_ids,
    self_weight,
    neighbour_weight,
    bias_vector,
):
    panels = rep_gather(features, REP_COUNT[0])
    everything = lax.all_gather(panels, "grp", axis=0, tiled=True)
    row_blocks, group_count, slot_count, tile_size, _ = tile_values.shape
    panel_rows = panels.shape[0]
    panel_blocks = panel_rows // tile_size
    local_rows = row_blocks * tile_size
    total_rows = everything.shape[0]

    positions = lax.broadcasted_iota(jnp.int32, (row_blocks, group_count, slot_count), 2)
    usable = positions < tile_counts[:, :, None]
    row_sums = jnp.sum(tile_values, axis=4, dtype=jnp.float32)
    degree = 1.0 + jnp.sum(
        jnp.where(usable[:, :, :, None], row_sums, jnp.float32(0.0)), axis=(1, 2)
    ).reshape(local_rows)

    block_iota = lax.broadcasted_iota(jnp.int32, (1, 1, 1, panel_blocks), 3)
    hits = (tile_columns[:, :, :, None] == block_iota) & usable[:, :, :, None]
    by_row = jnp.transpose(tile_values, (0, 3, 1, 2, 4))
    dense = jnp.zeros((row_blocks, tile_size, group_count, panel_blocks, tile_size), jnp.bfloat16)
    for slot in range(slot_count):
        dense = jnp.where(
            hits[:, None, :, slot, :, None], by_row[:, :, :, slot, None, :], dense
        )
    dense = dense.reshape(local_rows, total_rows)

    totals = jnp.dot(dense, everything, preferred_element_type=jnp.float32)
    own_rows = row_gather(everything, state_ids)
    neighbour = (totals / jnp.sqrt(degree)[:, None]).astype(jnp.bfloat16)
    activation = jnp.dot(own_rows, self_weight, preferred_element_type=jnp.float32)
    activation = activation + jnp.dot(
        neighbour, neighbour_weight, preferred_element_type=jnp.float32
    )
    activation = activation + bias_vector[None, :]
    return jnp.maximum(activation, 0.0).astype(jnp.bfloat16)


REP_COUNT = [8]


def solution(mesh):
    REP_COUNT[0] = mesh.shape["rep"]
    placed = (
        P(("grp", "rep"), None),
        P(("grp", "rep"), None, None, None, None),
        P(("grp", "rep"), None, None),
        P(("grp", "rep"), None),
        P(("grp", "rep")),
        P(),
        P(),
        P(),
    )
    return jax.shard_map(
        on_device, mesh=mesh, in_specs=placed, out_specs=P(("grp", "rep"), None), check_vma=False
    )
```
